32 devices in a mesh: gx: 8 (over y, x, core), gy: 4 (over z).
Axes of the slice: x: 2, y: 2, z: 4, core: 2. Of those that a mesh axis runs over, the one named last changes fastest.
Arguments:
- forcing: float32 [64, 64, 512], P('gx', 'gy'), may hold values from -5 to 5
- coefficient: float32 [64, 64, 512], P('gx', 'gy'), may hold values from 0.5 to 2
- guess: float32 [64, 64, 512], P('gx', 'gy'), may hold values from -3 to 3
Outputs:
- pressure: float32 [64, 64, 512], P('gx', 'gy')
- residual: float32 [64, 64, 512], P('gx', 'gy')
The draws below stay inside these ranges and needn't reach their ends.
All inputs are finite; a program needn't handle non-finite values.
Results may differ from the reference program's by a relative error of at most 0.000028.
Values sent between devices are 32-bit elements; how exact they have to be, the bound alone decides.
A program may use at most 64 MiB of HBM per device.

```python
import math
import jax
import jax.numpy as jnp

NZ = 512
CPRE = 3
CPOST = 2
CCOARSE = 4
NX = 64
NY = 64


def draw_forcing(key, part):
    first = jax.random.fold_in(key, 0)
    values = jnp.clip(jax.random.normal(first, (NX, NY, NZ), jnp.float32), -5.0, 5.0)
    return values.astype(jnp.float32)


def block_levels(own_key, dims, pieces, low, top_value):
    level = 1.0
    for axis_at, parts in pieces:
        heights = jax.random.uniform(jax.random.fold_in(jax.random.fold_in(own_key, 6), axis_at), (parts,), jnp.float32, low / len(pieces), top_value / len(pieces))
        level = level * jnp.repeat(jnp.exp(heights), dims[axis_at] // parts).reshape((-1,) + (1,) * (len(dims) - 1 - axis_at))
    return level


def normal_values(key, dims, spread, bound, cuts=(), held_as=jnp.bfloat16):
    factor_of = block_levels(key, dims, cuts, -0.22, 0.18) if cuts else 1.0
    array = jax.random.normal(key, dims, jnp.float32) * spread * factor_of
    return jnp.minimum(jnp.maximum(array, -bound), bound).astype(held_as)


def setup_inputs(seed: int = 0) -> dict:
    streams_of = jax.random.split(jax.random.key(seed), 4)
    forcing = draw_forcing(jax.random.fold_in(streams_of[3], 71), 0)
    coefficient = jnp.clip(jnp.exp(math.log(2.0) - 1.3862944 * jax.random.uniform(streams_of[1], (NX, NY, NZ), jnp.float32) ** block_levels(streams_of[1], (NX, NY, NZ), ((0, 8), (1, 4)), -0.2, 0.2)), 0.5, 2.0)
    guess = normal_values(streams_of[2], (NX, NY, NZ), 0.5, 3.0, ((0, 8), (1, 4)), jnp.float32)
    return {"forcing": forcing, "coefficient": coefficient, "guess": guess}


theta = 1.15
delta = 0.85


def laplace(padded):
    center = padded[1:-1, 1:-1, 1:-1]
    beside = padded[2:, 1:-1, 1:-1] + padded[:-2, 1:-1, 1:-1]
    beside = beside + padded[1:-1, 2:, 1:-1] + padded[1:-1, :-2, 1:-1]
    beside = beside + padded[1:-1, 1:-1, 2:] + padded[1:-1, 1:-1, :-2]
    return 6.0 * center - beside


def chebyshev(state, remain, passes, operator, inverse):
    sigma = theta / delta
    rho = 1.0 / sigma
    direction = inverse * remain / theta
    for step in range(passes):
        if step > 0:
            rho_next = 1.0 / (2.0 * sigma - rho)
            direction = (rho_next * rho) * direction + (2.0 * rho_next / delta) * (inverse * remain)
            rho = rho_next
        state = state + direction
        remain = remain - operator(direction)
    return state, remain


def reference(forcing, coefficient, guess):
    def fine_op(value):
        return coefficient * laplace(jnp.pad(coefficient * value, 1))

    inverse = 1.0 / (6.0 * coefficient * coefficient)
    remain = forcing - fine_op(guess)
    state, remain = chebyshev(guess, remain, CPRE, fine_op, inverse)
    sx, sy, sz = remain.shape
    coarse_rhs = remain.reshape(sx // 2, 2, sy // 2, 2, sz // 2, 2).sum(axis=(1, 3, 5))
    coarse_coef = coefficient.reshape(sx // 2, 2, sy // 2, 2, sz // 2, 2).sum(axis=(1, 3, 5)) / 8.0

    def coarse_op(value):
        return 4.0 * coarse_coef * laplace(jnp.pad(coarse_coef * value, 1))

    coarse_inverse = 1.0 / (24.0 * coarse_coef * coarse_coef)
    correction, unused = chebyshev(jnp.zeros_like(coarse_rhs), coarse_rhs, CCOARSE, coarse_op, coarse_inverse)
    fine_corr = jnp.repeat(jnp.repeat(jnp.repeat(correction, 2, axis=0), 2, axis=1), 2, axis=2)
    state = state + fine_corr
    remain = forcing - fine_op(state)
    state, remain = chebyshev(state, remain, CPOST, fine_op, inverse)
    return state, remain
```

```python
import functools

import jax
import jax.numpy as jnp
from jax import lax
from jax.experimental import pallas as pl
from jax.experimental.pallas import tpu as pltpu
from jax.sharding import PartitionSpec as P

CPRE = 3
CPOST = 2
CCOARSE = 4
theta = 1.15
delta = 0.85

ROW = 8
MU = CPRE + 1
MG = CPRE
MS = CPOST
MK = CPOST + 1
MC = (MK + 1) // 2
MR = CCOARSE - 1 + MC
XF = MU
XC = MR

AROUND = ((1, 0), (-1, 0), (0, 1), (0, -1), (1, 1), (1, -1), (-1, 1), (-1, -1))
FAR = ((2, 0), (-2, 0))
MESH = pl.DeviceIdType.MESH


def weights(passes):
    sigma = theta / delta
    rho = 1.0 / sigma
    out = [(0.0, 1.0 / (6.0 * theta))]
    for _ in range(1, passes):
        rho_next = 1.0 / (2.0 * sigma - rho)
        out.append((rho_next * rho, 2.0 * rho_next / delta / 6.0))
        rho = rho_next
    return out


def laplace(ref, p):
    center = ref[p]
    rows, depth = center.shape
    lane = lax.broadcasted_iota(jnp.int32, center.shape, 1)
    beside = ref[p - 1] + ref[p + 1]
    beside = beside + pltpu.roll(center, 1, 0) + pltpu.roll(center, rows - 1, 0)
    below = jnp.where(lane == 0, 0.0, pltpu.roll(center, 1, 1))
    above = jnp.where(lane == depth - 1, 0.0, pltpu.roll(center, depth - 1, 1))
    return 6.0 * center - (beside + below + above)


def kernel(
    forcing_hbm, coef_hbm, guess_hbm, pressure_ref, residual_ref,
    forcing, coef, guess, inv, state, u_ext, g_ext, k_ext, s_ext, r_ext, ea, eb,
    c_ext, sc, ca, cb, cu, fold, spread, in_sem, send_sem, recv_sem,
):
    nx, ny, nz = forcing.shape
    cx, cy, cz = nx // 2, ny // 2, nz // 2
    ix, iy = lax.axis_index("gx"), lax.axis_index("gy")
    px, py = lax.axis_size("gx"), lax.axis_size("gy")
    rows = ny + 2 * ROW
    crows = cy + 2 * ROW

    def exists(dx, dy):
        return (ix + dx >= 0) & (ix + dx < px) & (iy + dy >= 0) & (iy + dy < py)

    loads = [
        pltpu.make_async_copy(src, dst, in_sem.at[i])
        for i, (src, dst) in enumerate(
            ((coef_hbm, coef), (guess_hbm, guess), (forcing_hbm, forcing))
        )
    ]
    for load in loads:
        load.start()

    barrier = pltpu.get_barrier_semaphore()
    for dx, dy in AROUND + FAR:
        @pl.when(exists(dx, dy))
        def _():
            pl.semaphore_signal(barrier, inc=1, device_id=(ix + dx, iy + dy), device_id_type=MESH)

    def span(step, depth, first, count):
        if step == 0:
            return pl.ds(first, count), pl.ds(first, count)
        if step > 0:
            return pl.ds(first + count - depth, depth), pl.ds(first - depth, depth)
        return pl.ds(first, depth), pl.ds(first + count, depth)

    class Margin:
        def __init__(self, ref, base, depth, corner, first, count, tall):
            self.ref, self.base = ref, base
            self.depth, self.corner = depth, corner
            self.first, self.count, self.tall = first, count, tall
            self.dirs = AROUND

        def copy(self, i):
            dx, dy = self.dirs[i]
            if abs(dx) == 2:
                over = self.depth - self.count
                if dx > 0:
                    xs = pl.ds(self.first + self.count - over, over)
                    xd = pl.ds(self.first - self.depth, over)
                else:
                    xs = pl.ds(self.first, over)
                    xd = pl.ds(self.first + self.count + self.depth - over, over)
            else:
                deep = self.corner if dy != 0 else self.depth
                xs, xd = span(dx, min(deep, self.count), self.first, self.count)
            ys, yd = span(dy, ROW, ROW, self.tall)
            return pltpu.make_async_remote_copy(
                src_ref=self.ref.at[xs, ys, :],
                dst_ref=self.ref.at[xd, yd, :],
                send_sem=send_sem.at[self.base + i],
                recv_sem=recv_sem.at[self.base + i],
                device_id=(ix + dx, iy + dy),
                device_id_type=MESH,
            )

        def start(self):
            for i, (dx, dy) in enumerate(self.dirs):
                @pl.when(exists(dx, dy))
                def _():
                    self.copy(i).start()

        def arrive(self):
            for i, (dx, dy) in enumerate(self.dirs):
                @pl.when(exists(-dx, -dy))
                def _():
                    self.copy(i).wait_recv()

        def sent(self):
            for i, (dx, dy) in enumerate(self.dirs):
                @pl.when(exists(dx, dy))
                def _():
                    self.copy(i).wait_send()

    mu = Margin(u_ext, 0, MU, MU - 1, XF, nx, ny)
    mg = Margin(g_ext, 8, MG, MG - 1, XF, nx, ny)
    mk = Margin(k_ext, 16, MK, MK - 1, XF, nx, ny)
    ms = Margin(r_ext, 24, MS, MS - 1, XF, nx, ny)
    mc = Margin(c_ext, 32, MR, MR - 1, XC, cx, cy)
    mc.dirs = AROUND + FAR
    own = pl.ds(ROW, ny)
    cown = pl.ds(ROW, cy)

    def inside(p, first, count, tall, shape):
        glob = ix * count - first + p
        ok = (glob >= 0) & (glob < px * count)
        row = lax.broadcasted_iota(jnp.int32, shape, 0) + (iy * tall - ROW)
        low = jnp.where(ok, 0, py * tall)
        return (row >= low) & (row < py * tall)

    def planes(low, high, body):
        def step(p, carry):
            body(p)
            return carry
        lax.fori_loop(low, high, step, 0)

    loads[0].wait()
    loads[1].wait()
    loads[2].wait()

    def scale(p):
        c = coef[p]
        q = 1.0 / c
        inv[p] = q
        u = c * guess[p]
        u_ext[p + XF, own, :] = u
        state[p] = u
        g_ext[p + XF, own, :] = forcing[p] * q

    planes(0, nx, scale)
    peers = sum(jnp.where(exists(dx, dy), 1, 0) for dx, dy in AROUND + FAR)
    pl.semaphore_wait(barrier, peers)
    mu.start()
    mg.start()

    blocks = nz // 128
    take = (
        lax.broadcasted_iota(jnp.int32, (256, 128), 0) // 2
        == lax.broadcasted_iota(jnp.int32, (256, 128), 1)
    ).astype(jnp.float32)
    give = (
        lax.broadcasted_iota(jnp.int32, (128, 256), 1) // 2
        == lax.broadcasted_iota(jnp.int32, (128, 256), 0)
    ).astype(jnp.float32)
    exact = functools.partial(
        jnp.dot, precision=lax.Precision.HIGHEST, preferred_element_type=jnp.float32
    )

    def folded():
        out = []
        for b in range(0, blocks, 2):
            pair = [
                fold[b + i, pl.ds(0, cx * cy, stride=2), :]
                + fold[b + i, pl.ds(1, cx * cy, stride=2), :]
                for i in range(2)
            ]
            out.append(exact(jnp.concatenate(pair, axis=1), take))
        return jnp.concatenate(out, axis=1)

    def fill(value):
        for q in range(cx):
            total = value(2 * q) + value(2 * q + 1)
            for b in range(blocks):
                fold[b, pl.ds(q * ny, ny), :] = total[:, b * 128 : (b + 1) * 128]

    fill(lambda p: coef[p])
    coarse_inv = 1.0 / (folded() * 0.125)
    sc[...] = coarse_inv * 0.25

    for b in range(blocks // 2):
        wide = exact(coarse_inv[:, b * 128 : (b + 1) * 128], give)
        for i in range(2):
            piece = wide[:, i * 128 : (i + 1) * 128]
            fold[2 * b + i, pl.ds(0, cx * cy, stride=2), :] = piece
            fold[2 * b + i, pl.ds(1, cx * cy, stride=2), :] = piece
    for p in range(nx):
        part = [fold[b, pl.ds((p // 2) * ny, ny), :] for b in range(blocks)]
        k_ext[p + XF, own, :] = coef[p] * jnp.concatenate(part, axis=1)
    mk.start()

    mu.arrive()
    mg.arrive()

    shape = (rows, nz)
    pre = weights(CPRE)
    end = XF + nx
    mask_of = lambda p: inside(p, XF, nx, ny, shape)

    mu.sent()

    def clean(p):
        u_ext[p] = jnp.where(mask_of(p), u_ext[p], 0.0)

    planes(XF - MU, XF, clean)
    planes(end, end + MU, clean)
    if True:
        def clean_own(p):
            for at in (0, ROW + ny):
                row = lax.broadcasted_iota(jnp.int32, (ROW, nz), 0) + (iy * ny - ROW + at)
                ok = (row >= 0) & (row < py * ny)
                u_ext[p, pl.ds(at, ROW), :] = jnp.where(ok, u_ext[p, pl.ds(at, ROW), :], 0.0)
        planes(XF, end, clean_own)

    def first(p):
        s = jnp.where(mask_of(p), g_ext[p] - laplace(u_ext, p), 0.0)
        s_ext[p] = s
        ea[p] = pre[0][1] * s

    planes(XF - MG, end + MG, first)
    now, later = ea, eb
    for k in range(1, CPRE):
        wide = CPRE - k

        def pass_on(p, now=now, later=later, k=k):
            s = jnp.where(mask_of(p), s_ext[p] - laplace(now, p), 0.0)
            s_ext[p] = s
            later[p] = pre[k][0] * now[p] + pre[k][1] * s

        planes(XF - wide, end + wide, pass_on)

        def gather(p, now=now):
            state[p] = state[p] + now[p + XF, own, :]

        planes(0, nx, gather)
        now, later = later, now

    def last(p):
        s = s_ext[p] - laplace(now, p)
        s = s[ROW : ROW + ny]
        r_ext[p, own, :] = s
        q = p - XF
        state[q] = state[q] + now[p, own, :]

    planes(XF, end, last)

    fill(lambda p: coef[p] * r_ext[p + XF, own, :])
    rhs = folded() * sc[...]
    for q in range(cx):
        c_ext[q + XC, cown, :] = rhs[q * cy : (q + 1) * cy]
    mc.start()
    ms.start()
    mc.arrive()
    mc.sent()

    cshape = (crows, cz)
    post = weights(CCOARSE)
    cend = XC + cx
    cmask = lambda p: inside(p, XC, cx, cy, cshape)

    def cfirst(p):
        s = jnp.where(cmask(p), c_ext[p], 0.0)
        c_ext[p] = s
        e = post[0][1] * s
        ca[p] = e
        cu[p] = e

    planes(0, cend + MR, cfirst)
    cnow, clater = ca, cb
    for k in range(1, CCOARSE):
        wide = MR - k

        def cpass(p, cnow=cnow, clater=clater, k=k):
            s = jnp.where(cmask(p), c_ext[p] - laplace(cnow, p), 0.0)
            c_ext[p] = s
            e = post[k][0] * cnow[p] + post[k][1] * s
            clater[p] = e
            cu[p] = cu[p] + e

        planes(XC - wide, cend + wide, cpass)
        cnow, clater = clater, cnow

    cplanes = cx + 2 * MC
    corr = cu[XC - MC : XC - MC + cplanes].reshape(cplanes * crows, cz)
    for b in range(blocks // 2):
        wide = exact(corr[:, b * 128 : (b + 1) * 128], give)
        for i in range(2):
            piece = wide[:, i * 128 : (i + 1) * 128]
            spread[2 * b + i, pl.ds(0, cplanes * crows, stride=2), :] = piece
            spread[2 * b + i, pl.ds(1, cplanes * crows, stride=2), :] = piece
    mk.arrive()
    mk.sent()
    shift = XF - 2 * MC

    def correct(p):
        at = pl.multiple_of(((p - shift) // 2) * (2 * crows) + ROW, ROW)
        part = [spread[b, pl.ds(at, rows), :] for b in range(blocks)]
        w = jnp.where(mask_of(p), k_ext[p] * jnp.concatenate(part, axis=1), 0.0)
        ea[p] = w

    planes(XF - MK, end + MK, correct)
    ms.arrive()
    ms.sent()
    mg.sent()
    after = weights(CPOST)

    def again(p):
        s = jnp.where(mask_of(p), r_ext[p] - laplace(ea, p), 0.0)
        s_ext[p] = s
        eb[p] = after[0][1] * s

    planes(XF - MS, end + MS, again)

    def add(p):
        state[p] = state[p] + ea[p + XF, own, :] + eb[p + XF, own, :]

    planes(0, nx, add)

    def post_pass(p):
        s = jnp.where(mask_of(p), s_ext[p] - laplace(eb, p), 0.0)
        s_ext[p] = s
        ea[p] = after[1][0] * eb[p] + after[1][1] * s

    planes(XF - 1, end + 1, post_pass)

    def finish(p):
        s = s_ext[p] - laplace(ea, p)
        q = p - XF
        residual_ref[q] = s[ROW : ROW + ny] * coef[q]
        pressure_ref[q] = (state[q] + ea[p, own, :]) * inv[q]

    planes(XF, end, finish)


def per_device(forcing, coefficient, guess):
    nx, ny, nz = forcing.shape
    f32 = jnp.float32
    block = pltpu.VMEM((nx, ny, nz), f32)
    fine = pltpu.VMEM((nx + 2 * XF, ny + 2 * ROW, nz), f32)
    cx, cy, cz = nx // 2, ny // 2, nz // 2
    coarse = pltpu.VMEM((cx + 2 * XC, cy + 2 * ROW, cz), f32)
    blocks = nz // 128
    spread_rows = (cx + 2 * MC) * (cy + 2 * ROW) * 2
    return pl.pallas_call(
        kernel,
        name="leg",
        out_shape=[jax.ShapeDtypeStruct((nx, ny, nz), f32)] * 2,
        in_specs=[pl.BlockSpec(memory_space=pl.ANY)] * 3,
        out_specs=[pl.BlockSpec(memory_space=pltpu.VMEM)] * 2,
        scratch_shapes=[block] * 5
        + [fine] * 7
        + [coarse, pltpu.VMEM((cx * cy, cz), f32), coarse, coarse, coarse]
        + [pltpu.VMEM((blocks, cx * ny, 128), f32), pltpu.VMEM((blocks, spread_rows, 128), f32)]
        + [
            pltpu.SemaphoreType.DMA((3,)),
            pltpu.SemaphoreType.DMA((42,)),
            pltpu.SemaphoreType.DMA((42,)),
        ],
        compiler_params=pltpu.CompilerParams(collective_id=0, has_side_effects=True),
    )(forcing, coefficient, guess)


def solution(mesh):
    spec = P("gx", "gy", None)
    return jax.shard_map(
        per_device, mesh=mesh, in_specs=(spec,) * 3, out_specs=(spec,) * 2, check_vma=False
    )
```

```python
import functools

import jax
import jax.numpy as jnp
from jax import lax
from jax.experimental import pallas as pl
from jax.experimental.pallas import tpu as pltpu
from jax.sharding import PartitionSpec as P

CPRE = 3
CPOST = 2
CCOARSE = 4
theta = 1.15
delta = 0.85

LANES = 128
ROW = 8
MU = CPRE + 1
MG = CPRE
MS = CPOST
MK = CPOST + 1
MC = (MK + 1) // 2
MR = CCOARSE - 1 + MC
CLOW = 1
XF = MU
XC = MR

AROUND = ((1, 0), (-1, 0), (0, 1), (0, -1), (1, 1), (1, -1), (-1, 1), (-1, -1))
FAR = ((2, 0), (-2, 0))
MESH = pl.DeviceIdType.MESH


def weights(passes):
    sigma = theta / delta
    rho = 1.0 / sigma
    out = [(0.0, 1.0 / (6.0 * theta))]
    for _ in range(1, passes):
        rho_next = 1.0 / (2.0 * sigma - rho)
        out.append((rho_next * rho, 2.0 * rho_next / delta / 6.0))
        rho = rho_next
    return out


def laplace(ref, p, low, count, one):
    blocks = ref.shape[1]
    here = pl.ds(low, count)
    center = [ref[p, b, here, :] for b in range(blocks)]
    lane = lax.broadcasted_iota(jnp.int32, center[0].shape, 1)
    first, last = lane == 0, lane == LANES - 1
    up = [pltpu.roll(c, 1, 1) for c in center]
    down = [pltpu.roll(c, LANES - 1, 1) for c in center]
    out = []
    for b in range(blocks):
        below = jnp.where(first, up[b - 1] if b > 0 else 0.0, up[b])
        above = jnp.where(last, down[b + 1] if b + 1 < blocks else 0.0, down[b])
        beside = ref[p - 1, b, here, :] + ref[p + 1, b, here, :]
        along = ref[p, b, pl.ds(low - one, count), :] + ref[p, b, pl.ds(low + one, count), :]
        out.append(6.0 * center[b] - ((beside + along) + (below + above)))
    return out


def kernel(
    forcing_hbm, coef_hbm, guess_hbm, state_out, remain_out,
    forcing, coef, guess, state, u_ext, g_ext, k_ext, s_ext, r_ext, ea, eb,
    packed, landed, c_ext, cs, ca, cb, cu, sc, fold, spread, in_sem, send_sem, recv_sem,
):
    nx, ny, nz = forcing.shape
    cx, cy, cz = nx // 2, ny // 2, nz // 2
    ix, iy = lax.axis_index("gx"), lax.axis_index("gy")
    px, py = lax.axis_size("gx"), lax.axis_size("gy")
    rows = ny + 2 * ROW
    crows = cy + 2 * ROW
    blocks, cblocks = nz // LANES, cz // LANES
    one = jnp.minimum(ix + 1, 1)

    def exists(dx, dy):
        return (ix + dx >= 0) & (ix + dx < px) & (iy + dy >= 0) & (iy + dy < py)

    loads = [
        pltpu.make_async_copy(src, dst, in_sem.at[i])
        for i, (src, dst) in enumerate(
            ((coef_hbm, coef), (guess_hbm, guess), (forcing_hbm, forcing))
        )
    ]
    for load in loads:
        load.start()

    barrier = pltpu.get_barrier_semaphore()
    for dx, dy in AROUND + FAR:
        @pl.when(exists(dx, dy))
        def _():
            pl.semaphore_signal(barrier, inc=1, device_id=(ix + dx, iy + dy), device_id_type=MESH)

    def span(step, depth, first, count):
        if step == 0:
            return pl.ds(first, count), pl.ds(first, count)
        if step > 0:
            return pl.ds(first + count - depth, depth), pl.ds(first - depth, depth)
        return pl.ds(first, depth), pl.ds(first + count, depth)

    used = [0]

    class Copies:
        def __init__(self, items):
            self.items = [(used[0] + i,) + item for i, item in enumerate(items)]
            used[0] += len(items)

        def of(self, item):
            at, dx, dy, src, dst = item
            return pltpu.make_async_remote_copy(
                src_ref=src, dst_ref=dst, send_sem=send_sem.at[at], recv_sem=recv_sem.at[at],
                device_id=(ix + dx, iy + dy), device_id_type=MESH,
            )

        def start(self):
            for item in self.items:
                @pl.when(exists(item[1], item[2]))
                def _():
                    self.of(item).start()

        def arrive(self):
            for item in self.items:
                @pl.when(exists(-item[1], -item[2]))
                def _():
                    self.of(item).wait_recv()

        def sent(self):
            for item in self.items:
                @pl.when(exists(item[1], item[2]))
                def _():
                    self.of(item).wait_send()

    def margin(ref, depth, corner, first, count, tall, dirs):
        items = []
        for dx, dy in dirs:
            if abs(dx) == 2:
                over = depth - count
                if dx > 0:
                    xs, xd = pl.ds(first + count - over, over), pl.ds(first - depth, over)
                else:
                    xs, xd = pl.ds(first, over), pl.ds(first + count + depth - over, over)
            else:
                deep = corner if dy != 0 else depth
                xs, xd = span(dx, min(deep, count), first, count)
            ys, yd = span(dy, ROW, ROW, tall)
            items.append((dx, dy, ref.at[xs, :, ys, :], ref.at[xd, :, yd, :]))
        return items

    items = margin(u_ext, MU, 0, XF, nx, ny, AROUND[:2])
    items += margin(g_ext, MG, 0, XF, nx, ny, AROUND[:2])
    for dx, dy in AROUND[2:]:
        side = 0 if dy > 0 else 1
        xs, xd = span(dx, MU - 1, XF, nx)
        items.append((dx, dy, packed.at[side, xs], landed.at[side, xd]))
    m1 = Copies(items)
    mk = Copies(margin(k_ext, MK, MK - 1, XF, nx, ny, AROUND))
    ms = Copies(margin(r_ext, MS, MS - 1, XF, nx, ny, AROUND))
    mc = Copies(margin(c_ext, MR, MR - 1, XC, cx, cy, AROUND + FAR))
    own = pl.ds(ROW, ny)
    cown = pl.ds(ROW, cy)

    def rowclass(iy_first, count, total):
        row = lax.broadcasted_iota(jnp.int32, (count, LANES), 0) + iy_first
        return jnp.where((row >= 0) & (row < total), 0, 1)

    def plane_in(p, first, count):
        glob = ix * count - first + p
        return jnp.where((glob >= 0) & (glob < px * count), 1, 0)

    def planes(low, high, body, step=2):
        def at(i, carry):
            for j in range(step):
                body(low + i * step + j)
            return carry
        lax.fori_loop(0, (high - low) // step, at, 0)

    lanes = lambda b: slice(b * LANES, (b + 1) * LANES)
    end = XF + nx

    for load in loads:
        load.wait()
    low_half = lax.broadcasted_iota(jnp.int32, (ROW, LANES), 0) < ROW // 2

    def scale(p):
        for b in range(blocks):
            c = coef[p, :, lanes(b)]
            u = c * guess[p, :, lanes(b)]
            g = forcing[p, :, lanes(b)] / c
            u_ext[p + XF, b, own, :] = u
            state[p + XF, b] = u
            g_ext[p + XF, b, own, :] = g
            half = ROW // 2
            packed[0, p + XF, b] = jnp.where(low_half, pltpu.roll(u[ny - ROW :], half, 0), g[ny - ROW :])
            packed[1, p + XF, b] = jnp.where(low_half, u[:ROW], pltpu.roll(g[:ROW], half, 0))

    planes(0, nx, scale)
    peers = sum(jnp.where(exists(dx, dy), 1, 0) for dx, dy in AROUND + FAR)
    pl.semaphore_wait(barrier, peers)
    m1.start()

    take = (
        lax.broadcasted_iota(jnp.int32, (2 * LANES, LANES), 0) // 2
        == lax.broadcasted_iota(jnp.int32, (2 * LANES, LANES), 1)
    ).astype(jnp.float32)
    give = (
        lax.broadcasted_iota(jnp.int32, (LANES, 2 * LANES), 1) // 2
        == lax.broadcasted_iota(jnp.int32, (LANES, 2 * LANES), 0)
    ).astype(jnp.float32)
    exact = functools.partial(
        jnp.dot, precision=lax.Precision.HIGHEST, preferred_element_type=jnp.float32
    )

    def folded():
        out = []
        for b in range(0, blocks, 2):
            pair = [
                fold[b + i, pl.ds(0, cx * cy, stride=2), :]
                + fold[b + i, pl.ds(1, cx * cy, stride=2), :]
                for i in range(2)
            ]
            out.append(exact(jnp.concatenate(pair, axis=1), take))
        return out

    def fill(value):
        for q in range(cx):
            for b in range(blocks):
                fold[b, pl.ds(q * ny, ny), :] = value(2 * q, b) + value(2 * q + 1, b)

    def widen(pieces, ref, count):
        for b, piece in enumerate(pieces):
            wide = exact(piece, give)
            for i in range(2):
                ref[2 * b + i, pl.ds(0, count, stride=2), :] = wide[:, lanes(i)]
                ref[2 * b + i, pl.ds(1, count, stride=2), :] = wide[:, lanes(i)]

    fill(lambda p, b: coef[p, :, lanes(b)])
    inverse = [1.0 / (c * 0.125) for c in folded()]
    for b in range(cblocks):
        sc[b] = inverse[b] * 0.25
    widen(inverse, fold, cx * cy)
    for p in range(nx):
        for b in range(blocks):
            k_ext[p + XF, b, own, :] = coef[p, :, lanes(b)] * fold[b, pl.ds((p // 2) * ny, ny), :]
    mk.start()

    zero = jnp.zeros((ny, LANES), jnp.float32)
    for dx, at in ((-1, 0), (1, end)):
        @pl.when(jnp.logical_not(exists(dx, 0)))
        def _():
            for p in range(MU):
                for b in range(blocks):
                    u_ext[at + p, b, own, :] = zero
    m1.arrive()

    def unpack(p):
        inside = plane_in(p, XF, nx) > 0
        over = inside & exists(0, -1)
        under = inside & exists(0, 1)
        for b in range(blocks):
            a = landed[0, p, b]
            u_ext[p, b, pl.ds(0, ROW), :] = jnp.where(over, pltpu.roll(a, ROW // 2, 0), 0.0)
            g_ext[p, b, pl.ds(0, ROW), :] = a
            a = landed[1, p, b]
            u_ext[p, b, pl.ds(ny + ROW, ROW), :] = jnp.where(under, a, 0.0)
            g_ext[p, b, pl.ds(ny + ROW, ROW), :] = pltpu.roll(a, ROW // 2, 0)

    planes(0, end + XF, unpack)

    low, count = ROW // 2, ny + ROW
    here = pl.ds(low, count)
    kinds = rowclass(iy * ny - ROW + low, count, py * ny)
    pre = weights(CPRE)

    def masked(p, value):
        return jnp.where(kinds < plane_in(p, XF, nx), value, 0.0)

    def first(p):
        for b, lap in enumerate(laplace(u_ext, p, low, count, one)):
            s = masked(p, g_ext[p, b, here, :] - lap)
            s_ext[p, b, here, :] = s
            ea[p, b, here, :] = pre[0][1] * s

    planes(XF - MG, end + MG, first)
    now, later = ea, eb
    for k in range(1, CPRE):
        wide = CPRE - k

        def pass_on(p, now=now, later=later, k=k):
            for b, lap in enumerate(laplace(now, p, low, count, one)):
                s = masked(p, s_ext[p, b, here, :] - lap)
                s_ext[p, b, here, :] = s
                later[p, b, here, :] = pre[k][0] * now[p, b, here, :] + pre[k][1] * s
                state[p, b] = state[p, b] + now[p, b, own, :]

        planes(XF - wide, end + wide, pass_on)
        now, later = later, now

    def last(p):
        for b, lap in enumerate(laplace(now, p, ROW, ny, one)):
            r_ext[p, b, own, :] = s_ext[p, b, own, :] - lap
            state[p, b] = state[p, b] + now[p, b, own, :]

    planes(XF, end, last)

    fill(lambda p, b: coef[p, :, lanes(b)] * r_ext[p + XF, b, own, :])
    for b, rhs in enumerate(folded()):
        rhs = rhs * sc[b]
        for q in range(cx):
            c_ext[q + XC, b, cown, :] = rhs[q * cy : (q + 1) * cy]
    mc.start()
    ms.start()
    mc.arrive()

    clow, ccount = CLOW, crows - 2 * CLOW
    every = pl.ds(clow, ccount)
    post = weights(CCOARSE)
    cend = XC + cx
    ckinds = rowclass(iy * cy - ROW + clow, ccount, py * cy)

    def cmasked(p, value):
        return jnp.where(ckinds < plane_in(p, XC, cx), value, 0.0)

    def cfirst(p):
        for b in range(cblocks):
            s = cmasked(p, c_ext[p, b, every, :])
            cs[p, b, every, :] = s
            e = post[0][1] * s
            ca[p, b, every, :] = e
            cu[p, b, every, :] = e

    planes(0, cend + MR, cfirst)
    cnow, clater = ca, cb
    for k in range(1, CCOARSE):
        wide = MR - k

        def cpass(p, cnow=cnow, clater=clater, k=k):
            for b, lap in enumerate(laplace(cnow, p, clow, ccount, one)):
                s = cmasked(p, cs[p, b, every, :] - lap)
                cs[p, b, every, :] = s
                e = post[k][0] * cnow[p, b, every, :] + post[k][1] * s
                clater[p, b, every, :] = e
                cu[p, b, every, :] = cu[p, b, every, :] + e

        planes(XC - wide, cend + wide, cpass)
        cnow, clater = clater, cnow

    cplanes = cx + 2 * MC
    widen(
        [cu[XC - MC : XC - MC + cplanes, b].reshape(cplanes * crows, LANES) for b in range(cblocks)],
        spread, cplanes * crows,
    )
    mk.arrive()
    shift = XF - 2 * MC

    def correct(p):
        at = pl.multiple_of(((p - shift) // 2) * (2 * crows) + ROW, ROW)
        for b in range(blocks):
            w = k_ext[p, b, here, :] * spread[b, pl.ds(at + low, count), :]
            ea[p, b, here, :] = masked(p, w)

    planes(XF - MK, end + MK, correct)
    ms.arrive()
    after = weights(CPOST)

    def again(p):
        for b, lap in enumerate(laplace(ea, p, low, count, one)):
            s = masked(p, r_ext[p, b, here, :] - lap)
            s_ext[p, b, here, :] = s
            eb[p, b, here, :] = after[0][1] * s

    planes(XF - MS, end + MS, again)

    def post_pass(p):
        for b, lap in enumerate(laplace(eb, p, low, count, one)):
            s = masked(p, s_ext[p, b, here, :] - lap)
            s_ext[p, b, here, :] = s
            e = after[1][0] * eb[p, b, here, :] + after[1][1] * s
            state[p, b] = state[p, b] + ea[p, b, own, :] + eb[p, b, own, :]
            ea[p, b, here, :] = e

    planes(XF - 1, end + 1, post_pass)

    def finish(p):
        for b, lap in enumerate(laplace(ea, p, ROW, ny, one)):
            remain_out[p - XF, :, lanes(b)] = s_ext[p, b, own, :] - lap
            state_out[p - XF, :, lanes(b)] = state[p, b] + ea[p, b, own, :]

    planes(XF, end, finish)
    for copies in (m1, mk, ms, mc):
        copies.sent()


def per_device(forcing, coefficient, guess):
    nx, ny, nz = forcing.shape
    f32 = jnp.float32
    blocks = nz // LANES
    block = pltpu.VMEM((nx, ny, nz), f32)
    fine = pltpu.VMEM((nx + 2 * XF, blocks, ny + 2 * ROW, LANES), f32)
    kept = pltpu.VMEM((nx + 2 * XF, blocks, ny, LANES), f32)
    edge = pltpu.VMEM((2, nx + 2 * XF, blocks, ROW, LANES), f32)
    cx, cy = nx // 2, ny // 2
    coarse = pltpu.VMEM((cx + 2 * XC, blocks // 2, cy + 2 * ROW, LANES), f32)
    spread_rows = (cx + 2 * MC) * (cy + 2 * ROW) * 2
    state, remain = pl.pallas_call(
        kernel,
        name="leg",
        out_shape=[jax.ShapeDtypeStruct((nx, ny, nz), f32)] * 2,
        in_specs=[pl.BlockSpec(memory_space=pl.ANY)] * 3,
        out_specs=[pl.BlockSpec(memory_space=pltpu.VMEM)] * 2,
        scratch_shapes=[block] * 3
        + [kept]
        + [fine] * 7
        + [edge] * 2
        + [coarse] * 5
        + [pltpu.VMEM((blocks // 2, cx * cy, LANES), f32)]
        + [pltpu.VMEM((blocks, cx * ny, LANES), f32), pltpu.VMEM((blocks, spread_rows, LANES), f32)]
        + [
            pltpu.SemaphoreType.DMA((3,)),
            pltpu.SemaphoreType.DMA((36,)),
            pltpu.SemaphoreType.DMA((36,)),
        ],
        compiler_params=pltpu.CompilerParams(collective_id=0, has_side_effects=True),
    )(forcing, coefficient, guess)
    return state / coefficient, remain * coefficient


def solution(mesh):
    spec = P("gx", "gy", None)
    return jax.shard_map(
        per_device, mesh=mesh, in_specs=(spec,) * 3, out_specs=(spec,) * 2, check_vma=False
    )
```

```python
import functools

import jax
import jax.numpy as jnp
from jax import lax
from jax.experimental import pallas as pl
from jax.experimental.pallas import tpu as pltpu
from jax.sharding import PartitionSpec as P

CPRE = 3
CPOST = 2
CCOARSE = 4
theta = 1.15
delta = 0.85

LANES = 128
STEP = 14
WHOLE = 14
ROW = 8
MU = CPRE + 1
MG = CPRE
MS = CPOST
MK = CPOST + 1
MC = (MK + 1) // 2
MR = CCOARSE - 1 + MC
CLOW = 1
XF = MU
XC = MR

AROUND = ((1, 0), (-1, 0), (0, 1), (0, -1), (1, 1), (1, -1), (-1, 1), (-1, -1))
FAR = ((2, 0), (-2, 0))
MESH = pl.DeviceIdType.MESH


def weights(passes):
    sigma = theta / delta
    rho = 1.0 / sigma
    out = [(0.0, 1.0 / (6.0 * theta))]
    for _ in range(1, passes):
        rho_next = 1.0 / (2.0 * sigma - rho)
        out.append((rho_next * rho, 2.0 * rho_next / delta / 6.0))
        rho = rho_next
    return out


def laplace(ref, p, low, count, one):
    blocks = ref.shape[1]
    here = pl.ds(low, count)
    center = [ref[p, b, here, :] for b in range(blocks)]
    lane = lax.broadcasted_iota(jnp.int32, center[0].shape, 1)
    first, last = lane == 0, lane == LANES - 1
    up = [pltpu.roll(c, 1, 1) for c in center]
    down = [pltpu.roll(c, LANES - 1, 1) for c in center]
    out = []
    for b in range(blocks):
        below = jnp.where(first, up[b - 1] if b > 0 else 0.0, up[b])
        above = jnp.where(last, down[b + 1] if b + 1 < blocks else 0.0, down[b])
        beside = ref[p - 1, b, here, :] + ref[p + 1, b, here, :]
        along = ref[p, b, pl.ds(low - one, count), :] + ref[p, b, pl.ds(low + one, count), :]
        out.append(6.0 * center[b] - ((beside + along) + (below + above)))
    return out


def kernel(
    forcing_hbm, coef_hbm, guess_hbm, state_out, remain_out,
    forcing, coef, guess, state, u_ext, g_ext, k_ext, s_ext, r_ext, ea, eb, ec,
    packed, landed, c_ext, cs, ca, cb, cu, sc, fold, spread, in_sem, send_sem, recv_sem,
):
    nx, ny, nz = forcing.shape
    cx, cy, cz = nx // 2, ny // 2, nz // 2
    ix, iy = lax.axis_index("gx"), lax.axis_index("gy")
    px, py = lax.axis_size("gx"), lax.axis_size("gy")
    rows = ny + 2 * ROW
    crows = cy + 2 * ROW
    blocks, cblocks = nz // LANES, cz // LANES
    one = jnp.minimum(ix + 1, 1)

    def exists(dx, dy):
        return (ix + dx >= 0) & (ix + dx < px) & (iy + dy >= 0) & (iy + dy < py)

    loads = [
        pltpu.make_async_copy(src, dst, in_sem.at[i])
        for i, (src, dst) in enumerate(
            ((coef_hbm, coef), (guess_hbm, guess), (forcing_hbm, forcing))
        )
    ]
    for load in loads:
        load.start()

    barrier = pltpu.get_barrier_semaphore()
    for dx, dy in AROUND + FAR:
        @pl.when(exists(dx, dy))
        def _():
            pl.semaphore_signal(barrier, inc=1, device_id=(ix + dx, iy + dy), device_id_type=MESH)

    def span(step, depth, first, count):
        if step == 0:
            return pl.ds(first, count), pl.ds(first, count)
        if step > 0:
            return pl.ds(first + count - depth, depth), pl.ds(first - depth, depth)
        return pl.ds(first, depth), pl.ds(first + count, depth)

    used = [0]

    class Copies:
        def __init__(self, items):
            self.items = [(used[0] + i,) + item for i, item in enumerate(items)]
            used[0] += len(items)

        def of(self, item):
            at, dx, dy, src, dst = item
            return pltpu.make_async_remote_copy(
                src_ref=src, dst_ref=dst, send_sem=send_sem.at[at], recv_sem=recv_sem.at[at],
                device_id=(ix + dx, iy + dy), device_id_type=MESH,
            )

        def start(self):
            for item in self.items:
                @pl.when(exists(item[1], item[2]))
                def _():
                    self.of(item).start()

        def arrive(self):
            for item in self.items:
                @pl.when(exists(-item[1], -item[2]))
                def _():
                    self.of(item).wait_recv()

        def sent(self):
            for item in self.items:
                @pl.when(exists(item[1], item[2]))
                def _():
                    self.of(item).wait_send()

    def margin(ref, depth, corner, first, count, tall, dirs):
        items = []
        for dx, dy in dirs:
            if abs(dx) == 2:
                over = depth - count
                if dx > 0:
                    xs, xd = pl.ds(first + count - over, over), pl.ds(first - depth, over)
                else:
                    xs, xd = pl.ds(first, over), pl.ds(first + count + depth - over, over)
            else:
                deep = corner if dy != 0 else depth
                xs, xd = span(dx, min(deep, count), first, count)
            ys, yd = span(dy, ROW, ROW, tall)
            items.append((dx, dy, ref.at[xs, :, ys, :], ref.at[xd, :, yd, :]))
        return items

    def beside(dirs):
        items = []
        for dx, dy in dirs:
            side = 0 if dy > 0 else 1
            xs, xd = span(dx, MU - 1, XF, nx)
            items.append((dx, dy, packed.at[side, xs], landed.at[side, xd]))
        return items

    my = Copies(beside(AROUND[2:4]))
    m1 = Copies(
        margin(u_ext, MU, 0, XF, nx, ny, AROUND[:2])
        + margin(g_ext, MG, 0, XF, nx, ny, AROUND[:2])
        + beside(AROUND[4:])
    )
    mk = Copies(margin(k_ext, MK, MK - 1, XF, nx, ny, AROUND))
    ms = Copies(margin(r_ext, MS, MS - 1, XF, nx, ny, AROUND))
    mc = Copies(margin(c_ext, MR, MR - 1, XC, cx, cy, FAR + AROUND[4:] + AROUND[:4]))
    own = pl.ds(ROW, ny)
    cown = pl.ds(ROW, cy)

    def rowclass(iy_first, count, total):
        row = lax.broadcasted_iota(jnp.int32, (count, LANES), 0) + iy_first
        return jnp.where((row >= 0) & (row < total), 0, 1)

    def plane_in(p, first, count):
        glob = ix * count - first + p
        return jnp.where((glob >= 0) & (glob < px * count), 1, 0)

    def planes(low, high, body, step=STEP):
        if high <= low:
            return
        step = next(n for n in range(step, 0, -1) if (high - low) % n == 0)

        def at(i, carry):
            for j in range(step):
                body(low + i * step + j)
            return carry
        lax.fori_loop(0, (high - low) // step, at, 0)

    lanes = lambda b: slice(b * LANES, (b + 1) * LANES)
    end = XF + nx

    for load in loads:
        load.wait()
    low_half = lax.broadcasted_iota(jnp.int32, (ROW, LANES), 0) < ROW // 2

    def scale(p):
        for b in range(blocks):
            c = coef[p, :, lanes(b)]
            u = c * guess[p, :, lanes(b)]
            g = forcing[p, :, lanes(b)] / c
            u_ext[p + XF, b, own, :] = u
            state[p + XF, b] = u
            g_ext[p + XF, b, own, :] = g
            half = ROW // 2
            packed[0, p + XF, b] = jnp.where(low_half, pltpu.roll(u[ny - ROW :], half, 0), g[ny - ROW :])
            packed[1, p + XF, b] = jnp.where(low_half, u[:ROW], pltpu.roll(g[:ROW], half, 0))

    planes(0, nx, scale)
    peers = sum(jnp.where(exists(dx, dy), 1, 0) for dx, dy in AROUND + FAR)
    pl.semaphore_wait(barrier, peers)
    my.start()
    m1.start()

    take = (
        lax.broadcasted_iota(jnp.int32, (2 * LANES, LANES), 0) // 2
        == lax.broadcasted_iota(jnp.int32, (2 * LANES, LANES), 1)
    ).astype(jnp.float32)
    give = (
        lax.broadcasted_iota(jnp.int32, (LANES, 2 * LANES), 1) // 2
        == lax.broadcasted_iota(jnp.int32, (LANES, 2 * LANES), 0)
    ).astype(jnp.float32)
    exact = functools.partial(
        jnp.dot, precision=lax.Precision.HIGHEST, preferred_element_type=jnp.float32
    )

    def folded():
        out = []
        for b in range(0, blocks, 2):
            pair = [
                fold[b + i, pl.ds(0, cx * cy, stride=2), :]
                + fold[b + i, pl.ds(1, cx * cy, stride=2), :]
                for i in range(2)
            ]
            out.append(exact(jnp.concatenate(pair, axis=1), take))
        return out

    def fill(value):
        for q in range(cx):
            for b in range(blocks):
                fold[b, pl.ds(q * ny, ny), :] = value(2 * q, b) + value(2 * q + 1, b)

    def widen(pieces, ref, count):
        for b, piece in enumerate(pieces):
            wide = exact(piece, give)
            for i in range(2):
                ref[2 * b + i, pl.ds(0, count, stride=2), :] = wide[:, lanes(i)]
                ref[2 * b + i, pl.ds(1, count, stride=2), :] = wide[:, lanes(i)]

    fill(lambda p, b: coef[p, :, lanes(b)])
    inverse = [1.0 / (c * 0.125) for c in folded()]
    for b in range(cblocks):
        sc[b] = inverse[b] * 0.25
    widen(inverse, fold, cx * cy)
    for p in range(nx):
        for b in range(blocks):
            k_ext[p + XF, b, own, :] = coef[p, :, lanes(b)] * fold[b, pl.ds((p // 2) * ny, ny), :]
    mk.start()

    zero = jnp.zeros((ny, LANES), jnp.float32)
    for dx, at in ((-1, 0), (1, end)):
        @pl.when(jnp.logical_not(exists(dx, 0)))
        def _():
            for p in range(MU):
                for b in range(blocks):
                    u_ext[at + p, b, own, :] = zero
    def unpack(p):
        inside = plane_in(p, XF, nx) > 0
        over = inside & exists(0, -1)
        under = inside & exists(0, 1)
        for b in range(blocks):
            a = landed[0, p, b]
            u_ext[p, b, pl.ds(0, ROW), :] = jnp.where(over, pltpu.roll(a, ROW // 2, 0), 0.0)
            g_ext[p, b, pl.ds(0, ROW), :] = a
            a = landed[1, p, b]
            u_ext[p, b, pl.ds(ny + ROW, ROW), :] = jnp.where(under, a, 0.0)
            g_ext[p, b, pl.ds(ny + ROW, ROW), :] = pltpu.roll(a, ROW // 2, 0)

    low, count = ROW // 2, ny + ROW
    here = pl.ds(low, count)
    kinds = rowclass(iy * ny - ROW + low, count, py * ny)
    pre = weights(CPRE)

    def masked(p, value):
        return jnp.where(kinds < plane_in(p, XF, nx), value, 0.0)

    def first(p):
        for b, lap in enumerate(laplace(u_ext, p, low, count, one)):
            s = masked(p, g_ext[p, b, here, :] - lap)
            s_ext[p, b, here, :] = s
            ea[p, b, here, :] = pre[0][1] * s

    def pass_of(k):
        now, later = steps[k - 1], steps[k]

        def pass_on(p):
            for b, lap in enumerate(laplace(now, p, low, count, one)):
                s = masked(p, s_ext[p, b, here, :] - lap)
                s_ext[p, b, here, :] = s
                later[p, b, here, :] = pre[k][0] * now[p, b, here, :] + pre[k][1] * s
                state[p, b] = state[p, b] + now[p, b, own, :]

        return pass_on

    steps = (ea, eb, ec)
    stages = [first] + [pass_of(k) for k in range(1, CPRE)]
    inner = lambda k: min(k + 1, nx // 2)
    my.arrive()
    planes(XF, end, unpack)
    for k, stage in enumerate(stages):
        planes(XF + inner(k), end - inner(k), stage)
    m1.arrive()
    planes(0, XF, unpack)
    planes(end, end + XF, unpack)
    for k, stage in enumerate(stages):
        planes(XF - (CPRE - k), XF + inner(k), stage)
        planes(end - inner(k), end + (CPRE - k), stage)
    now = steps[CPRE - 1]

    def last(p):
        for b, lap in enumerate(laplace(now, p, ROW, ny, one)):
            r_ext[p, b, own, :] = s_ext[p, b, own, :] - lap
            state[p, b] = state[p, b] + now[p, b, own, :]

    planes(XF, end, last)

    fill(lambda p, b: coef[p, :, lanes(b)] * r_ext[p + XF, b, own, :])
    for b, rhs in enumerate(folded()):
        rhs = rhs * sc[b]
        for q in range(cx):
            c_ext[q + XC, b, cown, :] = rhs[q * cy : (q + 1) * cy]
    mc.start()
    ms.start()
    mc.arrive()

    clow, ccount = CLOW, crows - 2 * CLOW
    every = pl.ds(clow, ccount)
    post = weights(CCOARSE)
    cend = XC + cx
    ckinds = rowclass(iy * cy - ROW + clow, ccount, py * cy)

    def cmasked(p, value):
        return jnp.where(ckinds < plane_in(p, XC, cx), value, 0.0)

    def cfirst(p):
        for b in range(cblocks):
            s = cmasked(p, c_ext[p, b, every, :])
            cs[p, b, every, :] = s
            e = post[0][1] * s
            ca[p, b, every, :] = e
            cu[p, b, every, :] = e

    planes(0, cend + MR, cfirst, WHOLE)
    cnow, clater = ca, cb
    for k in range(1, CCOARSE):
        wide = MR - k

        def cpass(p, cnow=cnow, clater=clater, k=k):
            for b, lap in enumerate(laplace(cnow, p, clow, ccount, one)):
                s = cmasked(p, cs[p, b, every, :] - lap)
                cs[p, b, every, :] = s
                e = post[k][0] * cnow[p, b, every, :] + post[k][1] * s
                clater[p, b, every, :] = e
                cu[p, b, every, :] = cu[p, b, every, :] + e

        planes(XC - wide, cend + wide, cpass, WHOLE)
        cnow, clater = clater, cnow

    cplanes = cx + 2 * MC
    widen(
        [cu[XC - MC : XC - MC + cplanes, b].reshape(cplanes * crows, LANES) for b in range(cblocks)],
        spread, cplanes * crows,
    )
    mk.arrive()
    shift = XF - 2 * MC

    def correct(p):
        at = pl.multiple_of(((p - shift) // 2) * (2 * crows) + ROW, ROW)
        for b in range(blocks):
            w = k_ext[p, b, here, :] * spread[b, pl.ds(at + low, count), :]
            ea[p, b, here, :] = masked(p, w)

    planes(XF - MK, end + MK, correct)
    ms.arrive()
    after = weights(CPOST)

    def again(p):
        for b, lap in enumerate(laplace(ea, p, low, count, one)):
            s = masked(p, r_ext[p, b, here, :] - lap)
            s_ext[p, b, here, :] = s
            eb[p, b, here, :] = after[0][1] * s

    planes(XF - MS, end + MS, again)

    def post_pass(p):
        for b, lap in enumerate(laplace(eb, p, low, count, one)):
            s = masked(p, s_ext[p, b, here, :] - lap)
            s_ext[p, b, here, :] = s
            e = after[1][0] * eb[p, b, here, :] + after[1][1] * s
            state[p, b] = state[p, b] + ea[p, b, own, :] + eb[p, b, own, :]
            ea[p, b, here, :] = e

    planes(XF - 1, end + 1, post_pass)

    def finish(p):
        for b, lap in enumerate(laplace(ea, p, ROW, ny, one)):
            remain_out[p - XF, :, lanes(b)] = s_ext[p, b, own, :] - lap
            state_out[p - XF, :, lanes(b)] = state[p, b] + ea[p, b, own, :]

    planes(XF, end, finish)
    for copies in (my, m1, mk, ms, mc):
        copies.sent()


def per_device(forcing, coefficient, guess):
    nx, ny, nz = forcing.shape
    f32 = jnp.float32
    blocks = nz // LANES
    block = pltpu.VMEM((nx, ny, nz), f32)
    fine = pltpu.VMEM((nx + 2 * XF, blocks, ny + 2 * ROW, LANES), f32)
    kept = pltpu.VMEM((nx + 2 * XF, blocks, ny, LANES), f32)
    edge = pltpu.VMEM((2, nx + 2 * XF, blocks, ROW, LANES), f32)
    cx, cy = nx // 2, ny // 2
    coarse = pltpu.VMEM((cx + 2 * XC, blocks // 2, cy + 2 * ROW, LANES), f32)
    spread_rows = (cx + 2 * MC) * (cy + 2 * ROW) * 2
    state, remain = pl.pallas_call(
        kernel,
        name="leg",
        out_shape=[jax.ShapeDtypeStruct((nx, ny, nz), f32)] * 2,
        in_specs=[pl.BlockSpec(memory_space=pl.ANY)] * 3,
        out_specs=[pl.BlockSpec(memory_space=pltpu.VMEM)] * 2,
        scratch_shapes=[block] * 3
        + [kept]
        + [fine] * 8
        + [edge] * 2
        + [coarse] * 5
        + [pltpu.VMEM((blocks // 2, cx * cy, LANES), f32)]
        + [pltpu.VMEM((blocks, cx * ny, LANES), f32), pltpu.VMEM((blocks, spread_rows, LANES), f32)]
        + [
            pltpu.SemaphoreType.DMA((3,)),
            pltpu.SemaphoreType.DMA((36,)),
            pltpu.SemaphoreType.DMA((36,)),
        ],
        compiler_params=pltpu.CompilerParams(collective_id=0, has_side_effects=True),
    )(forcing, coefficient, guess)
    return state / coefficient, remain * coefficient


def solution(mesh):
    spec = P("gx", "gy", None)
    return jax.shard_map(
        per_device, mesh=mesh, in_specs=(spec,) * 3, out_specs=(spec,) * 2, check_vma=False
    )
```
